32 devices in a mesh: query: 8 (over z, y), store: 4 (over x, core).
Axes of the slice: x: 2, y: 2, z: 4, core: 2. Of those that a mesh axis runs over, the one named last changes fastest.
Arguments:
- in_rows: bfloat16 [8, 16384, 64], P('query', 'store'), may hold values from -6 to 6
- out_rows: bfloat16 [8, 16384, 128], P('query', 'store'), may hold values from -0.625 to 0.625
- row_doc: int32 [8, 16384], P('query', 'store'), may hold values from 0 to 31
- row_pos: int32 [8, 16384], P('query', 'store'), may hold values from 0 to 255
- doc_len: int32 [8, 128], P('query', 'store'), may hold values from 128 to 256
- eig_in: float32 [64], replicated, may hold values from 0.25 to 2
- eig_out: float32 [128], replicated, may hold values from 0.25 to 2
- basis_in: float32 [64, 64], replicated, may hold values from -0.75 to 0.75
- basis_out: float32 [128, 128], replicated, may hold values from -0.5 to 0.5
- train_feats: bfloat16 [8, 768, 8192], P('query', 'store'), may hold values from -0.0625 to 0.0625
Outputs:
- scores: bfloat16 [8, 128, 768], P('query', None, 'store')
The draws below stay inside these ranges and needn't reach their ends.
Inputs may be any that keep to these rules, and one draw needn't show every extreme that they name: On each device the 4096 rows form 8 blocks of 512 rows in order; the rows of block j belong to documents of group j in the same store column, and row_doc names the document among that destination's 32.
All inputs are finite; a program needn't handle non-finite values.
Results may differ from the reference program's by a relative error of at most 0.0049.
Values may be sent and summed in bfloat16 or wider, within the bound.
A program may use at most 64 MiB of HBM per device.

```python
import math
import jax
import jax.numpy as jnp
from jax import lax

DIN = 64
DOUT = 128
FEAT = 8192
DOCS_DEV = 32
RPD = 128
SLAB = 192
ROWS_DEV = 4096
CAP = 512
N_QUERY = 8
N_STORE = 4


def plant(drawn, rng, low, largest):
    extent = drawn.shape
    place = [jax.random.randint(jax.random.fold_in(rng, axis), (), 0, extent[axis]) for axis in range(len(extent))]
    drawn = drawn.at[tuple(place)].set(low)
    longest = extent.index(max(extent))
    place[longest] = (place[longest] + 1) % extent[longest]
    return drawn.at[tuple(place)].set(largest)


def shard_levels(rng, extent, pieces, low, top_value):
    def one(dim, blocks):
        steps = jax.random.uniform(jax.random.fold_in(jax.random.fold_in(rng, 6), dim), (blocks,), jnp.float32, low / len(pieces), top_value / len(pieces))
        return jnp.repeat(jnp.exp(steps), extent[dim] // blocks).reshape((-1,) + (1,) * (len(extent) - dim - 1))

    gain = one(*pieces[0])
    for cut in pieces[1:]:
        gain = gain * one(*cut)
    return gain


def normal_values(own_key, shape, width, limit, cuts=(), held_as=jnp.bfloat16):
    values = jax.random.normal(own_key, shape, jnp.float32) * width
    if len(cuts) > 0:
        values = shard_levels(own_key, shape, cuts, -0.22, 0.18) * values
    return jnp.clip(values, min=-limit, max=limit).astype(held_as)


def setup_inputs(seed: int = 0) -> dict:
    key_list = jax.random.split(jax.random.key(seed), 11)
    in_rows = normal_values(key_list[0], (N_QUERY, N_STORE * ROWS_DEV, DIN), 1.0, 6.0, ((0, 8), (1, 4)))
    out_rows = normal_values(key_list[1], (N_QUERY, N_STORE * ROWS_DEV, DOUT), 0.1, 0.625, ((0, 8), (1, 4)))
    row_doc = plant(jax.random.randint(key_list[2], (N_QUERY, N_STORE * ROWS_DEV), 0, DOCS_DEV), jax.random.fold_in(key_list[2], 1), 0, DOCS_DEV - 1).astype(jnp.int32)
    row_pos = plant(jax.random.randint(key_list[3], (N_QUERY, N_STORE * ROWS_DEV), 0, 2 * RPD), jax.random.fold_in(key_list[3], 1), 0, (2 * RPD) - 1).astype(jnp.int32)
    doc_len = plant(jax.random.randint(key_list[4], (N_QUERY, N_STORE * DOCS_DEV), RPD, 2 * RPD + 1), jax.random.fold_in(key_list[4], 1), RPD, 2 * RPD).astype(jnp.int32)
    eig_in = jnp.clip(jnp.exp(jax.random.uniform(key_list[5], (DIN,), jnp.float32, math.log(0.25), math.log(2.0))), 0.25, 2.0)
    eig_out = jnp.clip(jnp.exp(jax.random.uniform(key_list[6], (DOUT,), jnp.float32, math.log(0.25), math.log(2.0))), 0.25, 2.0)
    basis_in = normal_values(key_list[7], (DIN, DIN), DIN ** -0.5, 0.75, (), jnp.float32)
    basis_out = normal_values(key_list[8], (DOUT, DOUT), DOUT ** -0.5, 0.5, (), jnp.float32)
    train_feats = normal_values(key_list[9], (N_QUERY, N_STORE * SLAB, FEAT), FEAT ** -0.5, 0.0625, ((0, 8), (1, 4)))
    return {"in_rows": in_rows, "out_rows": out_rows, "row_doc": row_doc, "row_pos": row_pos, "doc_len": doc_len, "eig_in": eig_in, "eig_out": eig_out, "basis_in": basis_in, "basis_out": basis_out, "train_feats": train_feats}


damping = 0.1
highest = lax.Precision.HIGHEST


def collect(values, target):
    shaped = values.reshape((N_QUERY, N_STORE, N_QUERY, CAP) + values.shape[2:])
    picked = lax.dynamic_index_in_dim(shaped, target, 2, keepdims=False)
    picked = jnp.swapaxes(picked, 0, 1)
    return picked.reshape((N_STORE, N_QUERY * CAP) + values.shape[2:])


def precondition(gradients, scaling, basis_in, basis_out):
    doc_count = gradients.shape[1] // DIN
    rotated = jnp.dot(basis_out.T, gradients, precision=highest)
    turned = jnp.dot(rotated.reshape(DOUT * doc_count, DIN), basis_in, precision=highest)
    turned = turned.reshape(DOUT, doc_count, DIN) * scaling[:, None, :]
    restored = jnp.dot(basis_out, turned.reshape(DOUT, doc_count * DIN), precision=highest)
    final_map = jnp.dot(restored.reshape(DOUT * doc_count, DIN), basis_in.T, precision=highest)
    final_map = final_map.reshape(DOUT, doc_count, DIN)
    return jnp.transpose(final_map, (1, 0, 2)).reshape(doc_count, DOUT * DIN).astype(jnp.bfloat16)


def reference(in_rows, out_rows, row_doc, row_pos, doc_len, eig_in, eig_out, basis_in, basis_out, train_feats):
    scaling = 1.0 / (eig_out[:, None] * eig_in[None, :] + damping)

    def column_feats(operands):
        inputs_side, grads_side, docs_side, pos_side, lengths = operands
        live_mask = (docs_side[:, None] == jnp.arange(DOCS_DEV, dtype=jnp.int32)[None, :]) & (pos_side[:, None] < lengths[None, :])
        weights = live_mask.astype(jnp.float32)
        spread = (weights[:, :, None] * inputs_side.astype(jnp.float32)[:, None, :]).reshape(inputs_side.shape[0], DOCS_DEV * DIN)
        gradients = jnp.dot(grads_side.astype(jnp.float32).T, spread, precision=highest)
        return precondition(gradients, scaling, basis_in, basis_out)

    def score_group(target):
        inputs_all = collect(in_rows, target)
        grads_all = collect(out_rows, target)
        docs_all = collect(row_doc, target)
        pos_all = collect(row_pos, target)
        lengths = lax.dynamic_index_in_dim(doc_len, target, 0, keepdims=False).reshape(N_STORE, DOCS_DEV)
        features = lax.map(column_feats, (inputs_all, grads_all, docs_all, pos_all, lengths))
        queries = features.reshape(N_STORE * DOCS_DEV, FEAT)
        train_rows = lax.dynamic_index_in_dim(train_feats, target, 0, keepdims=False)
        result = jnp.dot(queries.astype(jnp.float32), train_rows.astype(jnp.float32).T, precision=highest)
        return result.astype(jnp.bfloat16)

    return lax.map(score_group, jnp.arange(N_QUERY, dtype=jnp.int32))
```

```python
import functools

import jax
import jax.numpy as jnp
from jax import lax
from jax.experimental import pallas as pl
from jax.experimental.pallas import tpu as pltpu
from jax.sharding import PartitionSpec as P

damping = 0.1
MESH = pl.DeviceIdType.MESH
f32 = jnp.float32
bf16 = jnp.bfloat16
CUT = 16
PLACES = 65536


def halves(x):
    high = x.astype(bf16)
    return high, (x - high.astype(f32)).astype(bf16)


def mm(a, b, ca, cb):
    return lax.dot_general(a, b, (((ca,), (cb,)), ((), ())), preferred_element_type=f32)


def kernel(
    queries, stores, x_ref, g_ref, doc_ref, pos_ref, len_hbm, eig_in_hbm, eig_out_hbm, bi_hbm, bo_hbm,
    train_ref, out_ref,
    len_ref, eig_in_ref, eig_out_ref, bi_ref, bo_ref, small_sem,
    x_own, doc_own, pos_own, x_turned, code_own,
    x_got, g_got, code_got, named_got, train, acc, feats,
    spread_in, scaling_ref, mixed, weighed, total,
    x_send, g_send, code_send, x_recv, g_recv, code_recv, own_sem, train_sem,
    far_send, far_recv, near_send, near_recv,
):
    me = lax.axis_index("query")
    column = lax.axis_index("store")
    chips = stores // 2
    chip, core = column // 2, column % 2
    partner = chip * 2 + (1 - core)
    cap = g_ref.shape[0] // queries
    in_width, out_width = bi_ref.shape[0], bo_ref.shape[0]
    docs = len_ref.shape[1]
    slab = train_ref.shape[0]
    chunks = in_width // CUT
    span = CUT * out_width

    barrier = pltpu.get_barrier_semaphore()
    middle = queries // 2
    order = [(middle + n) % queries for n in range(queries) if n != middle]
    for m in order:
        pl.semaphore_signal(
            barrier, inc=1, device_id={"query": (me + m) % queries}, device_id_type=MESH
        )
    for d in range(1, chips):
        pl.semaphore_signal(
            barrier, inc=1, device_id={"store": (chip + d) % chips * 2 + core}, device_id_type=MESH
        )
    pl.semaphore_signal(barrier, inc=1, device_id={"store": partner}, device_id_type=MESH)

    small_copies = [
        pltpu.make_async_copy(there, here, small_sem.at[n])
        for n, (there, here) in enumerate(
            (
                (bi_hbm, bi_ref),
                (x_ref, x_own),
                (doc_ref, doc_own),
                (pos_ref, pos_own),
                (len_hbm, len_ref),
                (eig_in_hbm, eig_in_ref),
                (eig_out_hbm, eig_out_ref),
                (bo_hbm, bo_ref),
            )
        )
    ]
    own_rows = pl.ds(pl.multiple_of(me * cap, cap), cap)
    g_copy = pltpu.make_async_copy(g_ref.at[own_rows], g_got.at[0], own_sem)
    train_copy = pltpu.make_async_copy(train_ref, train, train_sem)
    for copy in small_copies:
        copy.start()
    train_copy.start()
    g_copy.start()
    for copy in small_copies:
        copy.wait()

    code_own[...] = doc_own[...] * PLACES + pos_own[...]
    bi_high, bi_low = halves(bi_ref[...])
    turn = jnp.concatenate([bi_high, bi_low], axis=0)
    step = 512

    def rotate(n, carry):
        rows = pl.ds(pl.multiple_of(n * step, step), step)
        x = x_own[:, rows]
        x_turned[:, rows] = mm(turn, jnp.concatenate([x, x], axis=0), 0, 0).astype(bf16)
        return carry

    lax.fori_loop(0, x_own.shape[1] // step, rotate, 0)

    pl.semaphore_wait(barrier, (queries - 1) + (chips - 1) + 1)

    def head_copies(m):
        target = (me + m) % queries
        rows = pl.ds(pl.multiple_of(target * cap, cap), cap)
        there = {"query": target}
        return (
            pltpu.make_async_remote_copy(
                code_own.at[:, rows], code_got.at[m], code_send.at[m], code_recv.at[m],
                device_id=there, device_id_type=MESH,
            ),
            pltpu.make_async_remote_copy(
                g_ref.at[rows], g_got.at[m], g_send.at[m], g_recv.at[m],
                device_id=there, device_id_type=MESH,
            ),
        )

    def x_copy(m, c):
        target = (me + m) % queries
        rows = pl.ds(pl.multiple_of(target * cap, cap), cap)
        part = pl.ds(pl.multiple_of(c * CUT, CUT), CUT)
        return pltpu.make_async_remote_copy(
            x_turned.at[part, rows], x_got.at[m, part], x_send.at[m, c], x_recv.at[m, c],
            device_id={"query": target}, device_id_type=MESH,
        )

    def over_peers(body):
        def one(n, carry):
            body((middle + n) % queries)
            return carry

        lax.fori_loop(0, middle, one, 0)
        lax.fori_loop(middle + 1, queries, one, 0)

    def launch(m):
        for copy in head_copies(m):
            copy.start()

    over_peers(launch)
    for c in range(chunks):
        over_peers(lambda m, c=c: x_copy(m, c).start())

    bo = bo_ref[...]
    bt_high, bt_low = halves(bo.T)
    first = jnp.concatenate(
        [
            jnp.concatenate([bt_high, bt_high], axis=1),
            jnp.concatenate([bt_low, bt_low], axis=1),
        ],
        axis=0,
    )
    square = (in_width, in_width)
    diagonal = lax.broadcasted_iota(jnp.int32, square, 0) == lax.broadcasted_iota(
        jnp.int32, square, 1
    )
    eig_column = jnp.sum(
        jnp.where(diagonal, jnp.broadcast_to(eig_in_ref[...], square), 0.0), axis=1, keepdims=True
    )
    scaling_ref[...] = 1.0 / (eig_column * eig_out_ref[...] + damping)
    wide = 8 * in_width
    tall = jnp.broadcast_to(bi_ref[...].T[:, None, :], (in_width, 8, in_width)).reshape(wide, in_width)
    tall = jnp.concatenate([tall] * 8, axis=1)
    same = (
        lax.broadcasted_iota(jnp.int32, (wide, wide), 0) % 8
        == lax.broadcasted_iota(jnp.int32, (wide, wide), 1) // in_width
    )
    tall_high, tall_low = halves(jnp.where(same, tall, 0.0))
    spread_in[...] = jnp.concatenate([tall_high, tall_low], axis=1)

    train_copy.wait()

    def mix(b, carry):
        parts = []
        for h in range(2):
            block = train[:, pl.ds(pl.multiple_of((2 * b + h) * wide, wide), wide)]
            got = mm(spread_in[...], jnp.concatenate([block, block], axis=1), 1, 1)
            parts.append(got.reshape(in_width, 8, slab))
        high, low = halves(jnp.concatenate(parts, axis=1))
        mixed[:, pl.ds(pl.multiple_of(b * 16, 16), 16), :] = high
        mixed[:, pl.ds(pl.multiple_of(out_width + b * 16, 16), 16), :] = low
        return carry

    lax.fori_loop(0, out_width // 16, mix, 0)

    def weigh(i, carry):
        both = mm(first, mixed[i], 1, 0)
        high, low = halves(both[:out_width] + both[out_width:])
        scaled_high, scaled_low = halves(bo * scaling_ref[pl.ds(i, 1), :])
        last = jnp.concatenate(
            [
                jnp.concatenate([scaled_high, scaled_high], axis=1),
                jnp.concatenate([scaled_low, scaled_low], axis=1),
            ],
            axis=0,
        )
        both = mm(last, jnp.concatenate([high, low], axis=0), 1, 0)
        weighed[pl.ds(pl.multiple_of(i * out_width, out_width), out_width), :] = (
            both[:out_width] + both[out_width:]
        ).astype(bf16)
        return carry

    lax.fori_loop(0, in_width, weigh, 0, unroll=4)

    quarter = 8 * CUT

    def name(slot):
        code = code_got[slot]
        doc, place = code >> 16, code & (PLACES - 1)
        limit = jnp.zeros_like(doc)
        for e in range(docs):
            limit = jnp.where(doc == e, len_ref[0, e], limit)
        named = jnp.where(place < limit, doc, -1).astype(f32)
        named_got[slot] = jnp.broadcast_to(named, (16, cap)).astype(bf16)

    def absorb(slot, c, fresh):
        named = named_got[slot]
        inputs = x_got[slot, pl.ds(c * CUT, CUT), :]
        grads = g_got[slot]
        for start in range(0, docs, 8):
            spread = jnp.concatenate(
                [
                    jnp.where(named == jnp.asarray(e, bf16), inputs, jnp.zeros_like(inputs))
                    for e in range(start, start + 8)
                ],
                axis=0,
            )
            rows = pl.ds(start * CUT, quarter)
            added = mm(spread, grads, 1, 0)
            if fresh:
                acc[c, rows, :] = added
            else:
                acc[c, rows, :] += added

    def far_copy(d, c):
        columns = pl.ds(c * span, span)
        return pltpu.make_async_remote_copy(
            feats.at[0, :, columns], feats.at[2 * d, :, columns],
            far_send.at[d, c], far_recv.at[d, c],
            device_id={"store": (chip + d) % chips * 2 + core}, device_id_type=MESH,
        )

    def near_copy(d, c):
        columns = pl.ds(c * span, span)
        return pltpu.make_async_remote_copy(
            feats.at[2 * d, :, columns], feats.at[2 * d + 1, :, columns],
            near_send.at[d, c], near_recv.at[d, c],
            device_id={"store": partner}, device_id_type=MESH,
        )

    code_got[0] = code_own[:, own_rows]
    x_got[0] = x_turned[:, own_rows]
    g_copy.wait()
    name(0)
    for c in range(chunks):
        absorb(0, c, True)

    def forward(c):
        for d in range(1, chips):
            far_copy(d, c).wait_recv()
            near_copy(d, c).start()

    def score(c):
        for d in range(chips):
            near_copy(d, c).wait_recv()
        columns = pl.ds(c * span, span)
        queried = feats[:, :, columns].reshape(stores * docs, span)
        part = mm(queried, weighed[columns, :], 1, 0)
        if c == 0:
            total[...] = part
        else:
            total[...] += part

    for c in range(chunks):
        def arrive(m, c=c):
            if c == 0:
                for copy in head_copies(m):
                    copy.wait_recv()
                name(m)
            x_copy(m, c).wait_recv()
            absorb(m, c, False)

        over_peers(arrive)
        for i in range(CUT):
            feats[0, :, pl.ds(c * span + i * out_width, out_width)] = acc[
                c, pl.ds(i, docs, stride=CUT), :
            ].astype(bf16)
        for d in range(1, chips):
            far_copy(d, c).start()
        near_copy(0, c).start()
        if c > 0:
            forward(c - 1)
    for c in range(chunks - 1):
        score(c)
    forward(chunks - 1)
    score(chunks - 1)

    def put(slot, owner):
        start = pl.multiple_of(owner * docs, docs)
        out_ref[pl.ds(start, docs), :] = total[pl.ds(slot * docs, docs), :].astype(bf16)

    for d in range(chips):
        origin = (chip + chips - d) % chips * 2
        put(2 * d, origin + core)
        put(2 * d + 1, origin + (1 - core))

    def drain(m):
        for copy in head_copies(m):
            copy.wait_send()
        for c in range(chunks):
            x_copy(m, c).wait_send()

    over_peers(drain)
    for c in range(chunks):
        for d in range(1, chips):
            far_copy(d, c).wait_send()
        for d in range(chips):
            near_copy(d, c).wait_send()


def on_device(
    queries, stores,
    in_rows, out_rows, row_doc, row_pos, doc_len, eig_in, eig_out, basis_in, basis_out, train_feats,
):
    row_count, in_width = in_rows.shape[1:]
    out_width = out_rows.shape[2]
    docs = doc_len.shape[1]
    slab, feat = train_feats.shape[1:]
    cap = row_count // queries
    hbm = pl.BlockSpec(memory_space=pltpu.HBM)
    vmem = pl.BlockSpec(memory_space=pltpu.VMEM)
    dma = pltpu.SemaphoreType.DMA
    chips = stores // 2
    chunks = in_width // CUT
    scores = pl.pallas_call(
        functools.partial(kernel, queries, stores),
        name="attribution",
        out_shape=jax.ShapeDtypeStruct((stores * docs, slab), bf16),
        in_specs=[hbm] * 10,
        out_specs=vmem,
        scratch_shapes=[
            pltpu.SMEM((1, docs), jnp.int32),
            pltpu.VMEM((1, in_width), f32),
            pltpu.VMEM((1, out_width), f32),
            pltpu.VMEM((in_width, in_width), f32),
            pltpu.VMEM((out_width, out_width), f32),
            dma((8,)),
            pltpu.VMEM((in_width, row_count), bf16),
            pltpu.VMEM((1, row_count), jnp.int32),
            pltpu.VMEM((1, row_count), jnp.int32),
            pltpu.VMEM((in_width, row_count), bf16),
            pltpu.VMEM((1, row_count), jnp.int32),
            pltpu.VMEM((queries, in_width, cap), bf16),
            pltpu.VMEM((queries, cap, out_width), bf16),
            pltpu.VMEM((queries, 1, cap), jnp.int32),
            pltpu.VMEM((queries, 16, cap), bf16),
            pltpu.VMEM((slab, feat), bf16),
            pltpu.VMEM((chunks, docs * CUT, out_width), f32),
            pltpu.VMEM((stores, docs, feat), bf16),
            pltpu.VMEM((8 * in_width, 16 * in_width), bf16),
            pltpu.VMEM((in_width, out_width), f32),
            pltpu.VMEM((in_width, 2 * out_width, slab), bf16),
            pltpu.VMEM((feat, slab), bf16),
            pltpu.VMEM((stores * docs, slab), f32),
            dma((queries, chunks)), dma((queries,)), dma((queries,)),
            dma((queries, chunks)), dma((queries,)), dma((queries,)),
            dma, dma,
            *[dma((chips, chunks))] * 4,
        ],
        compiler_params=pltpu.CompilerParams(
            collective_id=0, has_side_effects=True, vmem_limit_bytes=67043328
        ),
    )(
        in_rows[0].T, out_rows[0], row_doc, row_pos, doc_len, eig_in[None], eig_out[None], basis_in, basis_out,
        train_feats[0],
    )
    return scores[None]


def solution(mesh):
    placed = (
        P("query", "store", None),
        P("query", "store", None),
        P("query", "store"),
        P("query", "store"),
        P("query", "store"),
        P(),
        P(),
        P(),
        P(),
        P("query", "store", None),
    )
    return jax.shard_map(
        functools.partial(on_device, mesh.shape["query"], mesh.shape["store"]),
        mesh=mesh, in_specs=placed, out_specs=P("query", None, "store"), check_vma=False,
    )
```

```python
import functools

import jax
import jax.numpy as jnp
from jax import lax
from jax.experimental import pallas as pl
from jax.experimental.pallas import tpu as pltpu
from jax.sharding import PartitionSpec as P

damping = 0.1
MESH = pl.DeviceIdType.MESH
f32 = jnp.float32
bf16 = jnp.bfloat16
CUT = 16
PLACES = 65536


def halves(x):
    high = x.astype(bf16)
    return high, (x - high.astype(f32)).astype(bf16)


def mm(a, b, ca, cb):
    return lax.dot_general(a, b, (((ca,), (cb,)), ((), ())), preferred_element_type=f32)


def kernel(
    queries, stores, x_ref, g_ref, doc_ref, pos_ref, len_hbm, eig_in_hbm, eig_out_hbm, bi_hbm, bo_hbm,
    train_ref, out_ref,
    len_ref, eig_in_ref, eig_out_ref, bi_ref, bo_ref, small_sem,
    x_own, doc_own, pos_own, x_turned, code_own,
    x_got, g_got, code_got, len_got, train, acc, feats, part_out, part_got,
    spread_in, scaling_ref, mixed, weighed, total,
    x_send, g_send, code_send, x_recv, g_recv, code_recv, own_sem, train_sem, len_sem,
    part_send, part_recv, far_send, far_recv, near_send, near_recv,
):
    me = lax.axis_index("query")
    column = lax.axis_index("store")
    chips = stores // 2
    chip, core = column // 2, column % 2
    partner = chip * 2 + (1 - core)
    direct, relayed = core == 0, core == 1
    cap = g_ref.shape[0] // queries
    in_width, out_width = bi_ref.shape[0], bo_ref.shape[0]
    docs = len_ref.shape[1]
    slab = train_ref.shape[0]
    chunks = in_width // CUT
    span = CUT * out_width
    half = queries // 2
    levels = [1 << b for b in range((queries - 1).bit_length())]

    def peer(m):
        return sum((me // level + m // level) % 2 * level for level in levels)

    barrier = pltpu.get_barrier_semaphore()
    for m in range(queries - 1, 0, -1):
        pl.semaphore_signal(barrier, inc=1, device_id={"query": peer(m)}, device_id_type=MESH)
    for d in range(1, chips):
        pl.semaphore_signal(
            barrier, inc=1, device_id={"store": (chip + d) % chips * 2 + core}, device_id_type=MESH
        )
    pl.semaphore_signal(barrier, inc=1, device_id={"store": partner}, device_id_type=MESH)

    small_copies = [
        pltpu.make_async_copy(there, here, small_sem.at[n])
        for n, (there, here) in enumerate(
            (
                (bi_hbm, bi_ref),
                (x_ref, x_own),
                (doc_ref, doc_own),
                (pos_ref, pos_own),
                (len_hbm, len_ref),
                (eig_in_hbm, eig_in_ref),
                (eig_out_hbm, eig_out_ref),
                (bo_hbm, bo_ref),
            )
        )
    ]

    def block_rows(m):
        return pl.ds(pl.multiple_of(peer(m) * cap, cap), cap)

    g_copy = pltpu.make_async_copy(g_ref.at[block_rows(0)], g_got.at[0], own_sem.at[0])
    g_pass = pltpu.make_async_copy(g_ref.at[block_rows(half)], g_got.at[half], own_sem.at[1])
    train_copy = pltpu.make_async_copy(train_ref, train, train_sem)
    for copy in small_copies:
        copy.start()
    train_copy.start()
    g_copy.start()
    for copy in small_copies:
        copy.wait()

    code_own[...] = doc_own[...] * PLACES + pos_own[...]
    bi_high, bi_low = halves(bi_ref[...])
    turn = jnp.concatenate([bi_high, bi_low], axis=0)
    step = 512

    def rotate(n, carry):
        rows = pl.ds(pl.multiple_of(n * step, step), step)
        x = x_own[:, rows]
        x_turned[:, rows] = mm(turn, jnp.concatenate([x, x], axis=0), 0, 0).astype(bf16)
        return carry

    lax.fori_loop(0, x_own.shape[1] // step, rotate, 0)

    pl.semaphore_wait(barrier, (queries - 1) + (chips - 1) + 1)

    def row_copies(m):
        rows = block_rows(m)
        there = {"query": peer(m - half * core * (m // (half + 1)))}
        return (
            pltpu.make_async_remote_copy(
                code_own.at[:, rows], code_got.at[m], code_send.at[m], code_recv.at[m],
                device_id=there, device_id_type=MESH,
            ),
            pltpu.make_async_remote_copy(
                g_ref.at[rows], g_got.at[m], g_send.at[m], g_recv.at[m],
                device_id=there, device_id_type=MESH,
            ),
            pltpu.make_async_remote_copy(
                x_turned.at[:, rows], x_got.at[m], x_send.at[m], x_recv.at[m],
                device_id=there, device_id_type=MESH,
            ),
        )

    len_copy = pltpu.make_async_remote_copy(
        len_ref, len_got, len_sem.at[0], len_sem.at[1],
        device_id={"query": peer(half)}, device_id_type=MESH,
    )

    def part_copy(c):
        return pltpu.make_async_remote_copy(
            part_out.at[c], part_got.at[c], part_send.at[c], part_recv.at[c],
            device_id={"query": peer(half)}, device_id_type=MESH,
        )

    def over(first, last, body):
        def one(n, carry):
            body(first - n)
            return carry

        lax.fori_loop(0, first - last + 1, one, 0)

    def launch(m):
        for copy in row_copies(m):
            copy.start()

    over(queries - 1, half + 1, launch)

    @pl.when(direct)
    def _():
        launch(half)

    @pl.when(relayed)
    def _():
        g_pass.start()
        len_copy.start()
        code_got[half] = code_own[:, block_rows(half)]
        x_got[half] = x_turned[:, block_rows(half)]

    code_got[0] = code_own[:, block_rows(0)]
    x_got[0] = x_turned[:, block_rows(0)]
    acc[1] = jnp.zeros(acc.shape[1:], f32)

    bo = bo_ref[...]
    bt_high, bt_low = halves(bo.T)
    first = jnp.concatenate(
        [
            jnp.concatenate([bt_high, bt_high], axis=1),
            jnp.concatenate([bt_low, bt_low], axis=1),
        ],
        axis=0,
    )
    def upright(row):
        square = (row.shape[1], row.shape[1])
        diagonal = lax.broadcasted_iota(jnp.int32, square, 0) == lax.broadcasted_iota(
            jnp.int32, square, 1
        )
        return jnp.sum(
            jnp.where(diagonal, jnp.broadcast_to(row, square), 0.0), axis=1, keepdims=True
        )

    scaling_ref[...] = 1.0 / (upright(eig_in_ref[...]) * eig_out_ref[...] + damping)
    wide = 8 * in_width
    tall = jnp.broadcast_to(bi_ref[...].T[:, None, :], (in_width, 8, in_width)).reshape(wide, in_width)
    tall = jnp.concatenate([tall] * 8, axis=1)
    same = (
        lax.broadcasted_iota(jnp.int32, (wide, wide), 0) % 8
        == lax.broadcasted_iota(jnp.int32, (wide, wide), 1) // in_width
    )
    tall_high, tall_low = halves(jnp.where(same, tall, 0.0))
    spread_in[...] = jnp.concatenate([tall_high, tall_low], axis=1)

    train_copy.wait()

    def mix(b, carry):
        parts = []
        for h in range(2):
            block = train[:, pl.ds(pl.multiple_of((2 * b + h) * wide, wide), wide)]
            got = mm(spread_in[...], jnp.concatenate([block, block], axis=1), 1, 1)
            parts.append(got.reshape(in_width, 8, slab))
        high, low = halves(jnp.concatenate(parts, axis=1))
        mixed[:, pl.ds(pl.multiple_of(b * 16, 16), 16), :] = high
        mixed[:, pl.ds(pl.multiple_of(out_width + b * 16, 16), 16), :] = low
        return carry

    lax.fori_loop(0, out_width // 16, mix, 0)
    over(half - 1, 1, launch)

    def weigh(i, carry):
        both = mm(first, mixed[i], 1, 0)
        high, low = halves(both[:out_width] + both[out_width:])
        scaled_high, scaled_low = halves(bo * scaling_ref[pl.ds(i, 1), :])
        last = jnp.concatenate(
            [
                jnp.concatenate([scaled_high, scaled_high], axis=1),
                jnp.concatenate([scaled_low, scaled_low], axis=1),
            ],
            axis=0,
        )
        both = mm(last, jnp.concatenate([high, low], axis=0), 1, 0)
        weighed[pl.ds(pl.multiple_of(i * out_width, out_width), out_width), :] = (
            both[:out_width] + both[out_width:]
        ).astype(bf16)
        return carry

    quarter = 8 * CUT

    def absorb(slot, side, limits, fresh=False):
        code = code_got[slot]
        doc, place = code >> 16, code & (PLACES - 1)
        listed = lax.broadcasted_iota(jnp.int32, (docs, cap), 0) == doc
        limit = jnp.sum(jnp.where(listed, limits, 0.0), axis=0, keepdims=True)
        named = jnp.where(place.astype(f32) < limit, doc.astype(f32), -1.0)
        named = jnp.broadcast_to(named, (16, cap)).astype(bf16)
        grads = g_got[slot]
        for start in range(0, docs, 8):
            kept = [named == jnp.asarray(e, bf16) for e in range(start, start + 8)]
            for c in range(chunks):
                inputs = x_got[slot, pl.ds(c * CUT, CUT), :]
                spread = jnp.concatenate(
                    [jnp.where(mask, inputs, jnp.zeros_like(inputs)) for mask in kept], axis=0
                )
                rows = pl.ds(start * CUT, quarter)
                added = mm(spread, grads, 1, 0)
                if fresh:
                    acc[side, c, rows, :] = added
                else:
                    acc[side, c, rows, :] += added

    def far_copy(d, c):
        columns = pl.ds(c * span, span)
        return pltpu.make_async_remote_copy(
            feats.at[0, :, columns], feats.at[2 * d, :, columns],
            far_send.at[d, c], far_recv.at[d, c],
            device_id={"store": (chip + d) % chips * 2 + core}, device_id_type=MESH,
        )

    def near_copy(d, c):
        columns = pl.ds(c * span, span)
        return pltpu.make_async_remote_copy(
            feats.at[2 * d, :, columns], feats.at[2 * d + 1, :, columns],
            near_send.at[d, c], near_recv.at[d, c],
            device_id={"store": partner}, device_id_type=MESH,
        )

    def forward(c):
        for d in range(1, chips):
            far_copy(d, c).wait_recv()
            near_copy(d, c).start()

    def score(c):
        for d in range(chips):
            near_copy(d, c).wait_recv()
        columns = pl.ds(c * span, span)
        queried = feats[:, :, columns].reshape(stores * docs, span)
        part = mm(queried, weighed[columns, :], 1, 0)
        if c == 0:
            total[...] = part
        else:
            total[...] += part

    def depart(c):
        for i in range(CUT):
            feats[0, :, pl.ds(c * span + i * out_width, out_width)] = acc[
                0, c, pl.ds(i, docs, stride=CUT), :
            ].astype(bf16)
        for d in range(1, chips):
            far_copy(d, c).start()
        near_copy(0, c).start()

    limits = upright(len_ref[...].astype(f32))

    def arrive(m, side, limits):
        for copy in row_copies(m):
            copy.wait_recv()
        absorb(m, side, limits)

    early = in_width // 2
    lax.fori_loop(0, early, weigh, 0, unroll=8)

    @pl.when(relayed)
    def _():
        len_copy.wait_recv()
        passed = upright(len_got[...].astype(f32))
        g_pass.wait()
        absorb(half, 1, passed)
        over(queries - 1, half + 1, lambda m: arrive(m, 1, passed))
        for c in range(chunks):
            part_out[c] = acc[1, c].astype(bf16)
            part_copy(c).start()

    lax.fori_loop(early, in_width, weigh, 0, unroll=8)
    g_copy.wait()
    absorb(0, 0, limits, True)
    over(half - 1, 1, lambda m: arrive(m, 0, limits))

    @pl.when(direct)
    def _():
        over(queries - 1, half, lambda m: arrive(m, 0, limits))
        for c in range(chunks):
            depart(c)
        for c in range(chunks):
            forward(c)
        for c in range(chunks):
            score(c)

    @pl.when(relayed)
    def _():
        for c in range(chunks):
            part_copy(c).wait_recv()
            acc[0, c] += part_got[c].astype(f32)
            depart(c)
            if c > 0:
                forward(c - 1)
            if c > 1:
                score(c - 2)
        forward(chunks - 1)
        for c in range(max(chunks - 2, 0), chunks):
            score(c)

    def put(slot, owner):
        start = pl.multiple_of(owner * docs, docs)
        out_ref[pl.ds(start, docs), :] = total[pl.ds(slot * docs, docs), :].astype(bf16)

    for d in range(chips):
        origin = (chip + chips - d) % chips * 2
        put(2 * d, origin + core)
        put(2 * d + 1, origin + (1 - core))

    def drain(m):
        for copy in row_copies(m):
            copy.wait_send()

    over(queries - 1, half + 1, drain)
    over(half - 1, 1, drain)

    @pl.when(direct)
    def _():
        drain(half)

    @pl.when(relayed)
    def _():
        len_copy.wait_send()
        for c in range(chunks):
            part_copy(c).wait_send()

    for c in range(chunks):
        for d in range(1, chips):
            far_copy(d, c).wait_send()
        for d in range(chips):
            near_copy(d, c).wait_send()


def on_device(
    queries, stores,
    in_rows, out_rows, row_doc, row_pos, doc_len, eig_in, eig_out, basis_in, basis_out, train_feats,
):
    row_count, in_width = in_rows.shape[1:]
    out_width = out_rows.shape[2]
    docs = doc_len.shape[1]
    slab, feat = train_feats.shape[1:]
    cap = row_count // queries
    hbm = pl.BlockSpec(memory_space=pltpu.HBM)
    vmem = pl.BlockSpec(memory_space=pltpu.VMEM)
    dma = pltpu.SemaphoreType.DMA
    chips = stores // 2
    chunks = in_width // CUT
    scores = pl.pallas_call(
        functools.partial(kernel, queries, stores),
        name="attribution",
        out_shape=jax.ShapeDtypeStruct((stores * docs, slab), bf16),
        in_specs=[hbm] * 10,
        out_specs=vmem,
        scratch_shapes=[
            pltpu.VMEM((1, docs), jnp.int32),
            pltpu.VMEM((1, in_width), f32),
            pltpu.VMEM((1, out_width), f32),
            pltpu.VMEM((in_width, in_width), f32),
            pltpu.VMEM((out_width, out_width), f32),
            dma((8,)),
            pltpu.VMEM((in_width, row_count), bf16),
            pltpu.VMEM((1, row_count), jnp.int32),
            pltpu.VMEM((1, row_count), jnp.int32),
            pltpu.VMEM((in_width, row_count), bf16),
            pltpu.VMEM((1, row_count), jnp.int32),
            pltpu.VMEM((queries, in_width, cap), bf16),
            pltpu.VMEM((queries, cap, out_width), bf16),
            pltpu.VMEM((queries, 1, cap), jnp.int32),
            pltpu.VMEM((1, docs), jnp.int32),
            pltpu.VMEM((slab, feat), bf16),
            pltpu.VMEM((2, chunks, docs * CUT, out_width), f32),
            pltpu.VMEM((stores, docs, feat), bf16),
            pltpu.VMEM((chunks, docs * CUT, out_width), bf16),
            pltpu.VMEM((chunks, docs * CUT, out_width), bf16),
            pltpu.VMEM((8 * in_width, 16 * in_width), bf16),
            pltpu.VMEM((in_width, out_width), f32),
            pltpu.VMEM((in_width, 2 * out_width, slab), bf16),
            pltpu.VMEM((feat, slab), bf16),
            pltpu.VMEM((stores * docs, slab), f32),
            dma((queries,)), dma((queries,)), dma((queries,)),
            dma((queries,)), dma((queries,)), dma((queries,)),
            dma((2,)), dma, dma((2,)),
            dma((chunks,)), dma((chunks,)),
            *[dma((chips, chunks))] * 4,
        ],
        compiler_params=pltpu.CompilerParams(
            collective_id=0, has_side_effects=True, vmem_limit_bytes=67043328
        ),
    )(
        in_rows[0].T, out_rows[0], row_doc, row_pos, doc_len, eig_in[None], eig_out[None], basis_in, basis_out,
        train_feats[0],
    )
    return scores[None]


def solution(mesh):
    placed = (
        P("query", "store", None),
        P("query", "store", None),
        P("query", "store"),
        P("query", "store"),
        P("query", "store"),
        P(),
        P(),
        P(),
        P(),
        P("query", "store", None),
    )
    return jax.shard_map(
        functools.partial(on_device, mesh.shape["query"], mesh.shape["store"]),
        mesh=mesh, in_specs=placed, out_specs=P("query", None, "store"), check_vma=False,
    )
```

```python
import functools

import jax
import jax.numpy as jnp
from jax import lax
from jax.experimental import pallas as pl
from jax.experimental.pallas import tpu as pltpu
from jax.sharding import PartitionSpec as P

damping = 0.1
MESH = pl.DeviceIdType.MESH
f32 = jnp.float32
bf16 = jnp.bfloat16
CUT = 16
PLACES = 65536


def halves(x):
    high = x.astype(bf16)
    return high, (x - high.astype(f32)).astype(bf16)


def mm(a, b, ca, cb):
    return lax.dot_general(a, b, (((ca,), (cb,)), ((), ())), preferred_element_type=f32)


def kernel(
    queries, stores, x_ref, g_ref, doc_ref, pos_ref, len_hbm, eig_in_hbm, eig_out_hbm, bi_hbm, bo_hbm,
    train_ref, out_ref,
    len_ref, eig_in_ref, eig_out_ref, bi_ref, bo_ref, small_sem,
    x_own, doc_own, pos_own, x_turned, code_own,
    x_got, g_got, code_got, len_got, train, acc, feats, part_out, part_got,
    spread_in, scaling_ref, mixed, weighed, total,
    x_send, g_send, code_send, x_recv, g_recv, code_recv, own_sem, train_sem, len_sem,
    part_send, part_recv, far_send, far_recv, near_send, near_recv,
):
    me = lax.axis_index("query")
    column = lax.axis_index("store")
    chips = stores // 2
    chip, core = column // 2, column % 2
    partner = chip * 2 + (1 - core)
    direct, relayed = core == 0, core == 1
    cap = g_ref.shape[0] // queries
    in_width, out_width = bi_ref.shape[0], bo_ref.shape[0]
    docs = len_ref.shape[1]
    slab = train_ref.shape[0]
    chunks = in_width // CUT
    span = CUT * out_width
    half = queries // 2
    levels = [1 << b for b in range((queries - 1).bit_length())]

    def peer(m):
        return sum((me // level + m // level) % 2 * level for level in levels)

    barrier = pltpu.get_barrier_semaphore()
    for m in range(queries - 1, 0, -1):
        pl.semaphore_signal(barrier, inc=1, device_id={"query": peer(m)}, device_id_type=MESH)
    for d in range(1, chips):
        pl.semaphore_signal(
            barrier, inc=1, device_id={"store": (chip + d) % chips * 2 + core}, device_id_type=MESH
        )
    pl.semaphore_signal(barrier, inc=1, device_id={"store": partner}, device_id_type=MESH)

    small_copies = [
        pltpu.make_async_copy(there, here, small_sem.at[n])
        for n, (there, here) in enumerate(
            (
                (bi_hbm, bi_ref),
                (x_ref, x_own),
                (doc_ref, doc_own),
                (pos_ref, pos_own),
                (len_hbm, len_ref),
                (eig_in_hbm, eig_in_ref),
                (eig_out_hbm, eig_out_ref),
                (bo_hbm, bo_ref),
            )
        )
    ]

    def block_rows(m):
        return pl.ds(pl.multiple_of(peer(m) * cap, cap), cap)

    g_copy = pltpu.make_async_copy(g_ref.at[block_rows(0)], g_got.at[0], own_sem.at[0])
    g_pass = pltpu.make_async_copy(g_ref.at[block_rows(half)], g_got.at[half], own_sem.at[1])
    train_copy = pltpu.make_async_copy(train_ref, train, train_sem)
    for copy in small_copies:
        copy.start()
    train_copy.start()
    g_copy.start()

    pl.semaphore_wait(barrier, (queries - 1) + (chips - 1) + 1)

    def row_copies(m):
        rows = block_rows(m)
        there = {"query": peer(m - half * core * (m // (half + 1)))}
        return (
            pltpu.make_async_remote_copy(
                code_own.at[:, rows], code_got.at[m], code_send.at[m], code_recv.at[m],
                device_id=there, device_id_type=MESH,
            ),
            pltpu.make_async_remote_copy(
                g_ref.at[rows], g_got.at[m], g_send.at[m], g_recv.at[m],
                device_id=there, device_id_type=MESH,
            ),
            pltpu.make_async_remote_copy(
                x_turned.at[:, rows], x_got.at[m], x_send.at[m], x_recv.at[m],
                device_id=there, device_id_type=MESH,
            ),
        )

    len_copy = pltpu.make_async_remote_copy(
        len_ref, len_got, len_sem.at[0], len_sem.at[1],
        device_id={"query": peer(half)}, device_id_type=MESH,
    )

    def part_copy(c):
        return pltpu.make_async_remote_copy(
            part_out.at[c], part_got.at[c], part_send.at[c], part_recv.at[c],
            device_id={"query": peer(half)}, device_id_type=MESH,
        )

    def over(first, last, body):
        def one(n, carry):
            body(first - n)
            return carry

        lax.fori_loop(0, first - last + 1, one, 0)

    def launch(m):
        for copy in row_copies(m):
            copy.start()

    def launch_grads(m):
        row_copies(m)[1].start()

    def launch_rest(m):
        code, _, inputs = row_copies(m)
        code.start()
        inputs.start()

    @pl.when(direct)
    def _():
        def one(n, carry):
            launch_grads(queries - 1 - n)
            launch_grads(half - 1 - n)
            return carry

        lax.fori_loop(0, half - 1, one, 0)
        launch_grads(half)

    @pl.when(relayed)
    def _():
        over(queries - 1, half + 1, launch_grads)
        over(half - 1, 1, launch_grads)

    for copy in small_copies:
        copy.wait()
    code_own[...] = doc_own[...] * PLACES + pos_own[...]
    bi_high, bi_low = halves(bi_ref[...])
    turn = jnp.concatenate([bi_high, bi_low], axis=0)
    step = 512

    def rotate(n, carry):
        rows = pl.ds(pl.multiple_of(n * step, step), step)
        x = x_own[:, rows]
        x_turned[:, rows] = mm(turn, jnp.concatenate([x, x], axis=0), 0, 0).astype(bf16)
        return carry

    lax.fori_loop(0, x_own.shape[1] // step, rotate, 0)


    @pl.when(direct)
    def _():
        def one(n, carry):
            launch_rest(queries - 1 - n)
            launch_rest(half - 1 - n)
            return carry

        lax.fori_loop(0, half - 1, one, 0)
        launch_rest(half)

    @pl.when(relayed)
    def _():
        over(queries - 1, half + 1, launch_rest)
        over(half - 1, 1, launch_rest)

    @pl.when(relayed)
    def _():
        g_pass.start()
        len_copy.start()
        code_got[half] = code_own[:, block_rows(half)]
        x_got[half] = x_turned[:, block_rows(half)]

    code_got[0] = code_own[:, block_rows(0)]
    x_got[0] = x_turned[:, block_rows(0)]
    acc[1] = jnp.zeros(acc.shape[1:], f32)

    bo = bo_ref[...]
    bt_high, bt_low = halves(bo.T)
    first = jnp.concatenate(
        [
            jnp.concatenate([bt_high, bt_high], axis=1),
            jnp.concatenate([bt_low, bt_low], axis=1),
        ],
        axis=0,
    )
    def upright(row):
        square = (row.shape[1], row.shape[1])
        diagonal = lax.broadcasted_iota(jnp.int32, square, 0) == lax.broadcasted_iota(
            jnp.int32, square, 1
        )
        return jnp.sum(
            jnp.where(diagonal, jnp.broadcast_to(row, square), 0.0), axis=1, keepdims=True
        )

    scaling_ref[...] = 1.0 / (upright(eig_in_ref[...]) * eig_out_ref[...] + damping)
    wide = 8 * in_width
    tall = jnp.broadcast_to(bi_ref[...].T[:, None, :], (in_width, 8, in_width)).reshape(wide, in_width)
    tall = jnp.concatenate([tall] * 8, axis=1)
    same = (
        lax.broadcasted_iota(jnp.int32, (wide, wide), 0) % 8
        == lax.broadcasted_iota(jnp.int32, (wide, wide), 1) // in_width
    )
    tall_high, tall_low = halves(jnp.where(same, tall, 0.0))
    spread_in[...] = jnp.concatenate([tall_high, tall_low], axis=1)

    train_copy.wait()

    def mix(b, carry):
        parts = []
        for h in range(2):
            block = train[:, pl.ds(pl.multiple_of((2 * b + h) * wide, wide), wide)]
            got = mm(spread_in[...], jnp.concatenate([block, block], axis=1), 1, 1)
            parts.append(got.reshape(in_width, 8, slab))
        high, low = halves(jnp.concatenate(parts, axis=1))
        mixed[:, pl.ds(pl.multiple_of(b * 16, 16), 16), :] = high
        mixed[:, pl.ds(pl.multiple_of(out_width + b * 16, 16), 16), :] = low
        return carry

    lax.fori_loop(0, out_width // 16, mix, 0)

    def weigh(i, carry):
        both = mm(first, mixed[i], 1, 0)
        high, low = halves(both[:out_width] + both[out_width:])
        scaled_high, scaled_low = halves(bo * scaling_ref[pl.ds(i, 1), :])
        last = jnp.concatenate(
            [
                jnp.concatenate([scaled_high, scaled_high], axis=1),
                jnp.concatenate([scaled_low, scaled_low], axis=1),
            ],
            axis=0,
        )
        both = mm(last, jnp.concatenate([high, low], axis=0), 1, 0)
        weighed[pl.ds(pl.multiple_of(i * out_width, out_width), out_width), :] = (
            both[:out_width] + both[out_width:]
        ).astype(bf16)
        return carry

    quarter = 8 * CUT

    def absorb(slot, side, limits, fresh=False):
        code = code_got[slot]
        doc, place = code >> 16, code & (PLACES - 1)
        listed = lax.broadcasted_iota(jnp.int32, (docs, cap), 0) == doc
        limit = jnp.sum(jnp.where(listed, limits, 0.0), axis=0, keepdims=True)
        named = jnp.where(place.astype(f32) < limit, doc.astype(f32), -1.0)
        named = jnp.broadcast_to(named, (16, cap)).astype(bf16)
        grads = g_got[slot]
        for start in range(0, docs, 8):
            kept = [named == jnp.asarray(e, bf16) for e in range(start, start + 8)]
            for c in range(chunks):
                inputs = x_got[slot, pl.ds(c * CUT, CUT), :]
                spread = jnp.concatenate(
                    [jnp.where(mask, inputs, jnp.zeros_like(inputs)) for mask in kept], axis=0
                )
                rows = pl.ds(start * CUT, quarter)
                added = mm(spread, grads, 1, 0)
                if fresh:
                    acc[side, c, rows, :] = added
                else:
                    acc[side, c, rows, :] += added

    def far_copy(d, c):
        columns = pl.ds(c * span, span)
        return pltpu.make_async_remote_copy(
            feats.at[0, :, columns], feats.at[2 * d, :, columns],
            far_send.at[d, c], far_recv.at[d, c],
            device_id={"store": (chip + d) % chips * 2 + core}, device_id_type=MESH,
        )

    def near_copy(d, c):
        columns = pl.ds(c * span, span)
        return pltpu.make_async_remote_copy(
            feats.at[2 * d, :, columns], feats.at[2 * d + 1, :, columns],
            near_send.at[d, c], near_recv.at[d, c],
            device_id={"store": partner}, device_id_type=MESH,
        )

    def forward(c):
        for d in range(1, chips):
            far_copy(d, c).wait_recv()
            near_copy(d, c).start()

    def score(c):
        for d in range(chips):
            near_copy(d, c).wait_recv()
        columns = pl.ds(c * span, span)
        queried = feats[:, :, columns].reshape(stores * docs, span)
        part = mm(queried, weighed[columns, :], 1, 0)
        if c == 0:
            total[...] = part
        else:
            total[...] += part

    def depart(c):
        for i in range(CUT):
            feats[0, :, pl.ds(c * span + i * out_width, out_width)] = acc[
                0, c, pl.ds(i, docs, stride=CUT), :
            ].astype(bf16)
        for d in range(1, chips):
            far_copy(d, c).start()
        near_copy(0, c).start()

    limits = upright(len_ref[...].astype(f32))

    def arrive(m, side, limits):
        for copy in row_copies(m):
            copy.wait_recv()
        absorb(m, side, limits)

    early = in_width // 2
    lax.fori_loop(0, early, weigh, 0, unroll=8)

    @pl.when(relayed)
    def _():
        len_copy.wait_recv()
        passed = upright(len_got[...].astype(f32))
        g_pass.wait()
        absorb(half, 1, passed)
        over(queries - 1, half + 1, lambda m: arrive(m, 1, passed))
        for c in range(chunks):
            part_out[c] = acc[1, c].astype(bf16)
            part_copy(c).start()

    lax.fori_loop(early, in_width, weigh, 0, unroll=8)
    g_copy.wait()
    absorb(0, 0, limits, True)
    over(half - 1, 1, lambda m: arrive(m, 0, limits))

    @pl.when(direct)
    def _():
        over(queries - 1, half, lambda m: arrive(m, 0, limits))
        for c in range(chunks):
            depart(c)
        for c in range(chunks):
            forward(c)
            if c > 0:
                score(c - 1)
        score(chunks - 1)

    @pl.when(relayed)
    def _():
        for c in range(chunks):
            part_copy(c).wait_recv()
            acc[0, c] += part_got[c].astype(f32)
            depart(c)
            if c > 0:
                forward(c - 1)
            if c > 1:
                score(c - 2)
        if chunks > 1:
            score(chunks - 2)
        forward(chunks - 1)
        score(chunks - 1)

    def put(slot, owner):
        start = pl.multiple_of(owner * docs, docs)
        out_ref[pl.ds(start, docs), :] = total[pl.ds(slot * docs, docs), :].astype(bf16)

    for d in range(chips):
        origin = (chip + chips - d) % chips * 2
        put(2 * d, origin + core)
        put(2 * d + 1, origin + (1 - core))

    def drain(m):
        for copy in row_copies(m):
            copy.wait_send()

    over(queries - 1, half + 1, drain)
    over(half - 1, 1, drain)

    @pl.when(direct)
    def _():
        drain(half)

    @pl.when(relayed)
    def _():
        len_copy.wait_send()
        for c in range(chunks):
            part_copy(c).wait_send()

    for c in range(chunks):
        for d in range(1, chips):
            far_copy(d, c).wait_send()
        for d in range(chips):
            near_copy(d, c).wait_send()


def on_device(
    queries, stores,
    in_rows, out_rows, row_doc, row_pos, doc_len, eig_in, eig_out, basis_in, basis_out, train_feats,
):
    row_count, in_width = in_rows.shape[1:]
    out_width = out_rows.shape[2]
    docs = doc_len.shape[1]
    slab, feat = train_feats.shape[1:]
    cap = row_count // queries
    hbm = pl.BlockSpec(memory_space=pltpu.HBM)
    vmem = pl.BlockSpec(memory_space=pltpu.VMEM)
    dma = pltpu.SemaphoreType.DMA
    chips = stores // 2
    chunks = in_width // CUT
    scores = pl.pallas_call(
        functools.partial(kernel, queries, stores),
        name="attribution",
        out_shape=jax.ShapeDtypeStruct((stores * docs, slab), bf16),
        in_specs=[hbm] * 10,
        out_specs=vmem,
        scratch_shapes=[
            pltpu.VMEM((1, docs), jnp.int32),
            pltpu.VMEM((1, in_width), f32),
            pltpu.VMEM((1, out_width), f32),
            pltpu.VMEM((in_width, in_width), f32),
            pltpu.VMEM((out_width, out_width), f32),
            dma((8,)),
            pltpu.VMEM((in_width, row_count), bf16),
            pltpu.VMEM((1, row_count), jnp.int32),
            pltpu.VMEM((1, row_count), jnp.int32),
            pltpu.VMEM((in_width, row_count), bf16),
            pltpu.VMEM((1, row_count), jnp.int32),
            pltpu.VMEM((queries, in_width, cap), bf16),
            pltpu.VMEM((queries, cap, out_width), bf16),
            pltpu.VMEM((queries, 1, cap), jnp.int32),
            pltpu.VMEM((1, docs), jnp.int32),
            pltpu.VMEM((slab, feat), bf16),
            pltpu.VMEM((2, chunks, docs * CUT, out_width), f32),
            pltpu.VMEM((stores, docs, feat), bf16),
            pltpu.VMEM((chunks, docs * CUT, out_width), bf16),
            pltpu.VMEM((chunks, docs * CUT, out_width), bf16),
            pltpu.VMEM((8 * in_width, 16 * in_width), bf16),
            pltpu.VMEM((in_width, out_width), f32),
            pltpu.VMEM((in_width, 2 * out_width, slab), bf16),
            pltpu.VMEM((feat, slab), bf16),
            pltpu.VMEM((stores * docs, slab), f32),
            dma((queries,)), dma((queries,)), dma((queries,)),
            dma((queries,)), dma((queries,)), dma((queries,)),
            dma((2,)), dma, dma((2,)),
            dma((chunks,)), dma((chunks,)),
            *[dma((chips, chunks))] * 4,
        ],
        compiler_params=pltpu.CompilerParams(
            collective_id=0, has_side_effects=True, vmem_limit_bytes=67043328
        ),
    )(
        in_rows[0].T, out_rows[0], row_doc, row_pos, doc_len, eig_in[None], eig_out[None], basis_in, basis_out,
        train_feats[0],
    )
    return scores[None]


def solution(mesh):
    placed = (
        P("query", "store", None),
        P("query", "store", None),
        P("query", "store"),
        P("query", "store"),
        P("query", "store"),
        P(),
        P(),
        P(),
        P(),
        P("query", "store", None),
    )
    return jax.shard_map(
        functools.partial(on_device, mesh.shape["query"], mesh.shape["store"]),
        mesh=mesh, in_specs=placed, out_specs=P("query", None, "store"), check_vma=False,
    )
```

```python
import functools

import jax
import jax.numpy as jnp
from jax import lax
from jax.experimental import pallas as pl
from jax.experimental.pallas import tpu as pltpu
from jax.sharding import PartitionSpec as P

damping = 0.1
MESH = pl.DeviceIdType.MESH
f32 = jnp.float32
bf16 = jnp.bfloat16
CUT = 16
PLACES = 65536


def halves(x):
    high = x.astype(bf16)
    return high, (x - high.astype(f32)).astype(bf16)


def mm(a, b, ca, cb):
    return lax.dot_general(a, b, (((ca,), (cb,)), ((), ())), preferred_element_type=f32)


def kernel(
    queries, stores, x_ref, g_ref, doc_ref, pos_ref, len_hbm, eig_in_hbm, eig_out_hbm, bi_hbm, bo_hbm,
    train_ref, out_ref,
    len_ref, eig_in_ref, eig_out_ref, bi_ref, bo_ref, small_sem,
    x_own, doc_own, pos_own, x_turned, code_own,
    x_got, g_got, code_got, len_got, train, acc, feats, part_out, part_got,
    spread_in, scaling_ref, mixed, weighed, total,
    x_send, g_send, code_send, x_recv, g_recv, code_recv, own_sem, train_sem, len_sem,
    part_send, part_recv, far_send, far_recv, near_send, near_recv,
):
    me = lax.axis_index("query")
    column = lax.axis_index("store")
    chips = stores // 2
    chip, core = column // 2, column % 2
    partner = chip * 2 + (1 - core)
    direct, relayed = core == 0, core == 1
    cap = g_ref.shape[0] // queries
    in_width, out_width = bi_ref.shape[0], bo_ref.shape[0]
    docs = len_ref.shape[1]
    slab = train_ref.shape[0]
    chunks = in_width // CUT
    span = CUT * out_width
    half = queries // 2
    levels = [1 << b for b in range((queries - 1).bit_length())]

    def peer(m):
        return sum((me // level + m // level) % 2 * level for level in levels)

    barrier = pltpu.get_barrier_semaphore()
    for m in range(queries - 1, 0, -1):
        pl.semaphore_signal(barrier, inc=1, device_id={"query": peer(m)}, device_id_type=MESH)
    for d in range(1, chips):
        pl.semaphore_signal(
            barrier, inc=1, device_id={"store": (chip + d) % chips * 2 + core}, device_id_type=MESH
        )
    pl.semaphore_signal(barrier, inc=1, device_id={"store": partner}, device_id_type=MESH)

    small_copies = [
        pltpu.make_async_copy(there, here, small_sem.at[n])
        for n, (there, here) in enumerate(
            (
                (bi_hbm, bi_ref),
                (x_ref, x_own),
                (doc_ref, doc_own),
                (pos_ref, pos_own),
                (len_hbm, len_ref),
                (eig_in_hbm, eig_in_ref),
                (eig_out_hbm, eig_out_ref),
                (bo_hbm, bo_ref),
            )
        )
    ]

    def block_rows(m):
        return pl.ds(pl.multiple_of(peer(m) * cap, cap), cap)

    g_copy = pltpu.make_async_copy(g_ref.at[block_rows(0)], g_got.at[0], own_sem.at[0])
    g_pass = pltpu.make_async_copy(g_ref.at[block_rows(half)], g_got.at[half], own_sem.at[1])
    train_copy = pltpu.make_async_copy(train_ref, train, train_sem)
    for copy in small_copies:
        copy.start()
    train_copy.start()
    g_copy.start()

    pl.semaphore_wait(barrier, (queries - 1) + (chips - 1) + 1)

    def row_copies(m):
        rows = block_rows(m)
        there = {"query": peer(m - half * core * (m // (half + 1)))}
        return (
            pltpu.make_async_remote_copy(
                code_own.at[:, rows], code_got.at[m], code_send.at[m], code_recv.at[m],
                device_id=there, device_id_type=MESH,
            ),
            pltpu.make_async_remote_copy(
                g_ref.at[rows], g_got.at[m], g_send.at[m], g_recv.at[m],
                device_id=there, device_id_type=MESH,
            ),
            pltpu.make_async_remote_copy(
                x_turned.at[:, rows], x_got.at[m], x_send.at[m], x_recv.at[m],
                device_id=there, device_id_type=MESH,
            ),
        )

    len_copy = pltpu.make_async_remote_copy(
        len_ref, len_got, len_sem.at[0], len_sem.at[1],
        device_id={"query": peer(half)}, device_id_type=MESH,
    )

    def part_copy(c):
        return pltpu.make_async_remote_copy(
            part_out.at[c], part_got.at[c], part_send.at[c], part_recv.at[c],
            device_id={"query": peer(half)}, device_id_type=MESH,
        )

    def over(first, last, body, unroll=1):
        def one(n, carry):
            body(first - n)
            return carry

        lax.fori_loop(0, first - last + 1, one, 0, unroll=unroll)

    def launch(m):
        for copy in row_copies(m):
            copy.start()

    def launch_grads(m):
        row_copies(m)[1].start()

    def launch_rest(m):
        code, _, inputs = row_copies(m)
        code.start()
        inputs.start()

    @pl.when(direct)
    def _():
        def one(n, carry):
            launch_grads(queries - 1 - n)
            launch_grads(half - 1 - n)
            return carry

        lax.fori_loop(0, half - 1, one, 0, unroll=3)
        launch_grads(half)

    @pl.when(relayed)
    def _():
        over(half - 1, 1, launch_grads, 3)
        over(queries - 1, half + 1, launch_grads, 3)

    for copy in small_copies:
        copy.wait()
    code_own[...] = doc_own[...] * PLACES + pos_own[...]
    bi_high, bi_low = halves(bi_ref[...])
    turn = jnp.concatenate([bi_high, bi_low], axis=0)
    step = 512

    def rotate(n, carry):
        rows = pl.ds(pl.multiple_of(n * step, step), step)
        x = x_own[:, rows]
        x_turned[:, rows] = mm(turn, jnp.concatenate([x, x], axis=0), 0, 0).astype(bf16)
        return carry

    lax.fori_loop(0, x_own.shape[1] // step, rotate, 0)


    @pl.when(direct)
    def _():
        def one(n, carry):
            launch_rest(queries - 1 - n)
            launch_rest(half - 1 - n)
            return carry

        lax.fori_loop(0, half - 1, one, 0, unroll=3)
        launch_rest(half)

    @pl.when(relayed)
    def _():
        over(queries - 1, half + 1, launch_rest, 3)
        over(half - 1, 1, launch_rest, 3)

    @pl.when(relayed)
    def _():
        g_pass.start()
        len_copy.start()
        code_got[half] = code_own[:, block_rows(half)]
        x_got[half] = x_turned[:, block_rows(half)]

    code_got[0] = code_own[:, block_rows(0)]
    x_got[0] = x_turned[:, block_rows(0)]
    acc[1] = jnp.zeros(acc.shape[1:], f32)

    bo = bo_ref[...]
    bt_high, bt_low = halves(bo.T)
    first = jnp.concatenate(
        [
            jnp.concatenate([bt_high, bt_high], axis=1),
            jnp.concatenate([bt_low, bt_low], axis=1),
        ],
        axis=0,
    )
    def upright(row):
        square = (row.shape[1], row.shape[1])
        diagonal = lax.broadcasted_iota(jnp.int32, square, 0) == lax.broadcasted_iota(
            jnp.int32, square, 1
        )
        return jnp.sum(
            jnp.where(diagonal, jnp.broadcast_to(row, square), 0.0), axis=1, keepdims=True
        )

    scaling_ref[...] = 1.0 / (upright(eig_in_ref[...]) * eig_out_ref[...] + damping)
    wide = 8 * in_width
    tall = jnp.broadcast_to(bi_ref[...].T[:, None, :], (in_width, 8, in_width)).reshape(wide, in_width)
    tall = jnp.concatenate([tall] * 8, axis=1)
    same = (
        lax.broadcasted_iota(jnp.int32, (wide, wide), 0) % 8
        == lax.broadcasted_iota(jnp.int32, (wide, wide), 1) // in_width
    )
    tall_high, tall_low = halves(jnp.where(same, tall, 0.0))
    spread_in[...] = jnp.concatenate([tall_high, tall_low], axis=1)

    train_copy.wait()

    def mix(b, carry):
        parts = []
        for h in range(2):
            block = train[:, pl.ds(pl.multiple_of((2 * b + h) * wide, wide), wide)]
            got = mm(spread_in[...], jnp.concatenate([block, block], axis=1), 1, 1)
            parts.append(got.reshape(in_width, 8, slab))
        high, low = halves(jnp.concatenate(parts, axis=1))
        mixed[:, pl.ds(pl.multiple_of(b * 16, 16), 16), :] = high
        mixed[:, pl.ds(pl.multiple_of(out_width + b * 16, 16), 16), :] = low
        return carry

    lax.fori_loop(0, out_width // 16, mix, 0)

    def weigh(i, carry):
        both = mm(first, mixed[i], 1, 0)
        high, low = halves(both[:out_width] + both[out_width:])
        scaled_high, scaled_low = halves(bo * scaling_ref[pl.ds(i, 1), :])
        last = jnp.concatenate(
            [
                jnp.concatenate([scaled_high, scaled_high], axis=1),
                jnp.concatenate([scaled_low, scaled_low], axis=1),
            ],
            axis=0,
        )
        both = mm(last, jnp.concatenate([high, low], axis=0), 1, 0)
        weighed[pl.ds(pl.multiple_of(i * out_width, out_width), out_width), :] = (
            both[:out_width] + both[out_width:]
        ).astype(bf16)
        return carry

    quarter = 8 * CUT

    def absorb(slot, side, limits, fresh=False):
        code = code_got[slot]
        doc, place = code >> 16, code & (PLACES - 1)
        listed = lax.broadcasted_iota(jnp.int32, (docs, cap), 0) == doc
        limit = jnp.sum(jnp.where(listed, limits, 0.0), axis=0, keepdims=True)
        named = jnp.where(place.astype(f32) < limit, doc.astype(f32), -1.0)
        named = jnp.broadcast_to(named, (16, cap)).astype(bf16)
        grads = g_got[slot]
        for start in range(0, docs, 8):
            kept = [named == jnp.asarray(e, bf16) for e in range(start, start + 8)]
            for c in range(chunks):
                inputs = x_got[slot, pl.ds(c * CUT, CUT), :]
                spread = jnp.concatenate(
                    [jnp.where(mask, inputs, jnp.zeros_like(inputs)) for mask in kept], axis=0
                )
                rows = pl.ds(start * CUT, quarter)
                added = mm(spread, grads, 1, 0)
                if fresh:
                    acc[side, c, rows, :] = added
                else:
                    acc[side, c, rows, :] += added

    def far_copy(d, c):
        columns = pl.ds(c * span, span)
        return pltpu.make_async_remote_copy(
            feats.at[0, :, columns], feats.at[2 * d, :, columns],
            far_send.at[d, c], far_recv.at[d, c],
            device_id={"store": (chip + d) % chips * 2 + core}, device_id_type=MESH,
        )

    def near_copy(d, c):
        columns = pl.ds(c * span, span)
        return pltpu.make_async_remote_copy(
            feats.at[2 * d, :, columns], feats.at[2 * d + 1, :, columns],
            near_send.at[d, c], near_recv.at[d, c],
            device_id={"store": partner}, device_id_type=MESH,
        )

    def forward(c):
        for d in range(1, chips):
            far_copy(d, c).wait_recv()
            near_copy(d, c).start()

    def score_chip(d, c):
        columns = pl.ds(c * span, span)
        near_copy(d, c).wait_recv()
        queried = feats[pl.ds(2 * d, 2), :, columns].reshape(2 * docs, span)
        part = mm(queried, weighed[columns, :], 1, 0)
        rows = pl.ds(2 * d * docs, 2 * docs)
        if c == 0:
            total[rows, :] = part
        else:
            total[rows, :] += part

    def score(c):
        for d in range(chips):
            near_copy(d, c).wait_recv()
        columns = pl.ds(c * span, span)
        queried = feats[:, :, columns].reshape(stores * docs, span)
        part = mm(queried, weighed[columns, :], 1, 0)
        if c == 0:
            total[...] = part
        else:
            total[...] += part

    def depart(c):
        for i in range(CUT):
            feats[0, :, pl.ds(c * span + i * out_width, out_width)] = acc[
                0, c, pl.ds(i, docs, stride=CUT), :
            ].astype(bf16)
        for d in range(1, chips):
            far_copy(d, c).start()
        near_copy(0, c).start()

    limits = upright(len_ref[...].astype(f32))

    def arrive(m, side, limits):
        for copy in row_copies(m):
            copy.wait_recv()
        absorb(m, side, limits)

    g_copy.wait()
    absorb(0, 0, limits, True)
    early = in_width // 4 * 3
    lax.fori_loop(0, early, weigh, 0, unroll=8)

    @pl.when(relayed)
    def _():
        len_copy.wait_recv()
        passed = upright(len_got[...].astype(f32))
        g_pass.wait()
        absorb(half, 1, passed)
        over(queries - 1, half + 1, lambda m: arrive(m, 1, passed))
        for c in range(chunks):
            part_out[c] = acc[1, c].astype(bf16)
            part_copy(c).start()

    lax.fori_loop(early, in_width, weigh, 0, unroll=8)
    over(half - 1, 1, lambda m: arrive(m, 0, limits))

    @pl.when(direct)
    def _():
        over(queries - 1, half, lambda m: arrive(m, 0, limits))
        for c in range(chunks):
            depart(c)
        for c in range(chunks):
            forward(c)
            if c > 0:
                score(c - 1)
        score(chunks - 1)

    @pl.when(relayed)
    def _():
        for c in range(chunks):
            part_copy(c).wait_recv()
            acc[0, c] += part_got[c].astype(f32)
            depart(c)
        for c in range(chunks - 1):
            forward(c)
            if c > 0:
                score(c - 1)
        if chunks > 1:
            score(chunks - 2)
        score_chip(0, chunks - 1)
        forward(chunks - 1)
        for d in range(1, chips):
            score_chip(d, chunks - 1)

    def put(slot, owner):
        start = pl.multiple_of(owner * docs, docs)
        out_ref[pl.ds(start, docs), :] = total[pl.ds(slot * docs, docs), :].astype(bf16)

    for d in range(chips):
        origin = (chip + chips - d) % chips * 2
        put(2 * d, origin + core)
        put(2 * d + 1, origin + (1 - core))

    def drain(m):
        for copy in row_copies(m):
            copy.wait_send()

    over(queries - 1, half + 1, drain)
    over(half - 1, 1, drain)

    @pl.when(direct)
    def _():
        drain(half)

    @pl.when(relayed)
    def _():
        len_copy.wait_send()
        for c in range(chunks):
            part_copy(c).wait_send()

    for c in range(chunks):
        for d in range(1, chips):
            far_copy(d, c).wait_send()
        for d in range(chips):
            near_copy(d, c).wait_send()


def on_device(
    queries, stores,
    in_rows, out_rows, row_doc, row_pos, doc_len, eig_in, eig_out, basis_in, basis_out, train_feats,
):
    row_count, in_width = in_rows.shape[1:]
    out_width = out_rows.shape[2]
    docs = doc_len.shape[1]
    slab, feat = train_feats.shape[1:]
    cap = row_count // queries
    hbm = pl.BlockSpec(memory_space=pltpu.HBM)
    vmem = pl.BlockSpec(memory_space=pltpu.VMEM)
    dma = pltpu.SemaphoreType.DMA
    chips = stores // 2
    chunks = in_width // CUT
    scores = pl.pallas_call(
        functools.partial(kernel, queries, stores),
        name="attribution",
        out_shape=jax.ShapeDtypeStruct((stores * docs, slab), bf16),
        in_specs=[hbm] * 10,
        out_specs=vmem,
        scratch_shapes=[
            pltpu.VMEM((1, docs), jnp.int32),
            pltpu.VMEM((1, in_width), f32),
            pltpu.VMEM((1, out_width), f32),
            pltpu.VMEM((in_width, in_width), f32),
            pltpu.VMEM((out_width, out_width), f32),
            dma((8,)),
            pltpu.VMEM((in_width, row_count), bf16),
            pltpu.VMEM((1, row_count), jnp.int32),
            pltpu.VMEM((1, row_count), jnp.int32),
            pltpu.VMEM((in_width, row_count), bf16),
            pltpu.VMEM((1, row_count), jnp.int32),
            pltpu.VMEM((queries, in_width, cap), bf16),
            pltpu.VMEM((queries, cap, out_width), bf16),
            pltpu.VMEM((queries, 1, cap), jnp.int32),
            pltpu.VMEM((1, docs), jnp.int32),
            pltpu.VMEM((slab, feat), bf16),
            pltpu.VMEM((2, chunks, docs * CUT, out_width), f32),
            pltpu.VMEM((stores, docs, feat), bf16),
            pltpu.VMEM((chunks, docs * CUT, out_width), bf16),
            pltpu.VMEM((chunks, docs * CUT, out_width), bf16),
            pltpu.VMEM((8 * in_width, 16 * in_width), bf16),
            pltpu.VMEM((in_width, out_width), f32),
            pltpu.VMEM((in_width, 2 * out_width, slab), bf16),
            pltpu.VMEM((feat, slab), bf16),
            pltpu.VMEM((stores * docs, slab), f32),
            dma((queries,)), dma((queries,)), dma((queries,)),
            dma((queries,)), dma((queries,)), dma((queries,)),
            dma((2,)), dma, dma((2,)),
            dma((chunks,)), dma((chunks,)),
            *[dma((chips, chunks))] * 4,
        ],
        compiler_params=pltpu.CompilerParams(
            collective_id=0, has_side_effects=True, vmem_limit_bytes=67043328
        ),
    )(
        in_rows[0].T, out_rows[0], row_doc, row_pos, doc_len, eig_in[None], eig_out[None], basis_in, basis_out,
        train_feats[0],
    )
    return scores[None]


def solution(mesh):
    placed = (
        P("query", "store", None),
        P("query", "store", None),
        P("query", "store"),
        P("query", "store"),
        P("query", "store"),
        P(),
        P(),
        P(),
        P(),
        P("query", "store", None),
    )
    return jax.shard_map(
        functools.partial(on_device, mesh.shape["query"], mesh.shape["store"]),
        mesh=mesh, in_specs=placed, out_specs=P("query", None, "store"), check_vma=False,
    )
```

```python
import functools

import jax
import jax.numpy as jnp
from jax import lax
from jax.experimental import pallas as pl
from jax.experimental.pallas import tpu as pltpu
from jax.sharding import PartitionSpec as P

damping = 0.1
MESH = pl.DeviceIdType.MESH
f32 = jnp.float32
bf16 = jnp.bfloat16
CUT = 16
PLACES = 65536


def halves(x):
    high = x.astype(bf16)
    return high, (x - high.astype(f32)).astype(bf16)


def mm(a, b, ca, cb):
    return lax.dot_general(a, b, (((ca,), (cb,)), ((), ())), preferred_element_type=f32)


def kernel(
    queries, stores, x_ref, g_ref, doc_ref, pos_ref, len_hbm, eig_in_hbm, eig_out_hbm, bi_hbm, bo_hbm,
    train_ref, out_ref,
    len_ref, eig_in_ref, eig_out_ref, bi_ref, bo_ref, small_sem,
    x_own, doc_own, pos_own, x_turned, code_own,
    x_got, g_got, code_got, len_got, train, acc, feats, part_out, part_got,
    spread_in, scaling_ref, mixed, weighed, total,
    x_send, g_send, code_send, x_recv, g_recv, code_recv, own_sem, train_sem, len_sem,
    part_send, part_recv, far_send, far_recv, near_send, near_recv,
):
    me = lax.axis_index("query")
    column = lax.axis_index("store")
    chips = stores // 2
    chip, core = column // 2, column % 2
    partner = chip * 2 + (1 - core)
    direct, relayed = core == 0, core == 1
    cap = g_ref.shape[0] // queries
    in_width, out_width = bi_ref.shape[0], bo_ref.shape[0]
    docs = len_ref.shape[1]
    slab = train_ref.shape[0]
    chunks = in_width // CUT
    span = CUT * out_width
    half = queries // 2
    levels = [1 << b for b in range((queries - 1).bit_length())]

    def peer(m):
        return sum((me // level + m // level) % 2 * level for level in levels)

    barrier = pltpu.get_barrier_semaphore()
    for m in range(queries - 1, 0, -1):
        pl.semaphore_signal(barrier, inc=1, device_id={"query": peer(m)}, device_id_type=MESH)
    for d in range(1, chips):
        pl.semaphore_signal(
            barrier, inc=1, device_id={"store": (chip + d) % chips * 2 + core}, device_id_type=MESH
        )
    pl.semaphore_signal(barrier, inc=1, device_id={"store": partner}, device_id_type=MESH)

    small_copies = [
        pltpu.make_async_copy(there, here, small_sem.at[n])
        for n, (there, here) in enumerate(
            (
                (bi_hbm, bi_ref),
                (x_ref, x_own),
                (doc_ref, doc_own),
                (pos_ref, pos_own),
                (len_hbm, len_ref),
                (eig_in_hbm, eig_in_ref),
                (eig_out_hbm, eig_out_ref),
                (bo_hbm, bo_ref),
            )
        )
    ]

    def block_rows(m):
        return pl.ds(pl.multiple_of(peer(m) * cap, cap), cap)

    g_copy = pltpu.make_async_copy(g_ref.at[block_rows(0)], g_got.at[0], own_sem.at[0])
    g_pass = pltpu.make_async_copy(g_ref.at[block_rows(half)], g_got.at[half], own_sem.at[1])
    train_copy = pltpu.make_async_copy(train_ref, train, train_sem)
    for copy in small_copies:
        copy.start()
    train_copy.start()
    g_copy.start()

    pl.semaphore_wait(barrier, (queries - 1) + (chips - 1) + 1)

    def row_copies(m):
        rows = block_rows(m)
        there = {"query": peer(m - half * core * (m // (half + 1)))}
        return (
            pltpu.make_async_remote_copy(
                code_own.at[:, rows], code_got.at[m], code_send.at[m], code_recv.at[m],
                device_id=there, device_id_type=MESH,
            ),
            pltpu.make_async_remote_copy(
                g_ref.at[rows], g_got.at[m], g_send.at[m], g_recv.at[m],
                device_id=there, device_id_type=MESH,
            ),
            pltpu.make_async_remote_copy(
                x_turned.at[:, rows], x_got.at[m], x_send.at[m], x_recv.at[m],
                device_id=there, device_id_type=MESH,
            ),
        )

    len_copy = pltpu.make_async_remote_copy(
        len_ref, len_got, len_sem.at[0], len_sem.at[1],
        device_id={"query": peer(half)}, device_id_type=MESH,
    )

    def part_copy(c):
        return pltpu.make_async_remote_copy(
            part_out.at[c], part_got.at[c], part_send.at[c], part_recv.at[c],
            device_id={"query": peer(half)}, device_id_type=MESH,
        )

    def over(first, last, body, unroll=1):
        def one(n, carry):
            body(first - n)
            return carry

        lax.fori_loop(0, first - last + 1, one, 0, unroll=unroll)

    def launch(m):
        for copy in row_copies(m):
            copy.start()

    def launch_grads(m):
        row_copies(m)[1].start()

    def launch_rest(m):
        code, _, inputs = row_copies(m)
        code.start()
        inputs.start()

    @pl.when(direct)
    def _():
        def one(n, carry):
            launch_grads(queries - 1 - n)
            launch_grads(half - 1 - n)
            return carry

        lax.fori_loop(0, half - 1, one, 0, unroll=3)
        launch_grads(half)

    @pl.when(relayed)
    def _():
        over(half - 1, 1, launch_grads, 3)
        over(queries - 1, half + 1, launch_grads, 3)

    for copy in small_copies:
        copy.wait()
    code_own[...] = doc_own[...] * PLACES + pos_own[...]
    bi_high, bi_low = halves(bi_ref[...])
    turn = jnp.concatenate([bi_high, bi_low], axis=0)
    step = 512

    def rotate(n, carry):
        rows = pl.ds(pl.multiple_of(n * step, step), step)
        x = x_own[:, rows]
        x_turned[:, rows] = mm(turn, jnp.concatenate([x, x], axis=0), 0, 0).astype(bf16)
        return carry

    lax.fori_loop(0, x_own.shape[1] // step, rotate, 0)


    @pl.when(direct)
    def _():
        def one(n, carry):
            launch_rest(queries - 1 - n)
            launch_rest(half - 1 - n)
            return carry

        lax.fori_loop(0, half - 1, one, 0, unroll=3)
        launch_rest(half)

    @pl.when(relayed)
    def _():
        over(queries - 1, half + 1, launch_rest, 3)
        over(half - 1, 1, launch_rest, 3)

    @pl.when(relayed)
    def _():
        g_pass.start()
        len_copy.start()
        code_got[half] = code_own[:, block_rows(half)]
        x_got[half] = x_turned[:, block_rows(half)]

    code_got[0] = code_own[:, block_rows(0)]
    x_got[0] = x_turned[:, block_rows(0)]
    acc[1] = jnp.zeros(acc.shape[1:], f32)

    bo = bo_ref[...]
    bt_high, bt_low = halves(bo.T)
    first = jnp.concatenate(
        [
            jnp.concatenate([bt_high, bt_high], axis=1),
            jnp.concatenate([bt_low, bt_low], axis=1),
        ],
        axis=0,
    )
    def upright(row):
        square = (row.shape[1], row.shape[1])
        diagonal = lax.broadcasted_iota(jnp.int32, square, 0) == lax.broadcasted_iota(
            jnp.int32, square, 1
        )
        return jnp.sum(
            jnp.where(diagonal, jnp.broadcast_to(row, square), 0.0), axis=1, keepdims=True
        )

    scaling_ref[...] = 1.0 / (upright(eig_in_ref[...]) * eig_out_ref[...] + damping)
    wide = 8 * in_width
    tall = jnp.broadcast_to(bi_ref[...].T[:, None, :], (in_width, 8, in_width)).reshape(wide, in_width)
    tall = jnp.concatenate([tall] * 8, axis=1)
    same = (
        lax.broadcasted_iota(jnp.int32, (wide, wide), 0) % 8
        == lax.broadcasted_iota(jnp.int32, (wide, wide), 1) // in_width
    )
    tall_high, tall_low = halves(jnp.where(same, tall, 0.0))
    spread_in[...] = jnp.concatenate([tall_high, tall_low], axis=1)

    train_copy.wait()

    def mix(b, carry):
        parts = []
        for h in range(2):
            block = train[:, pl.ds(pl.multiple_of((2 * b + h) * wide, wide), wide)]
            got = mm(spread_in[...], jnp.concatenate([block, block], axis=1), 1, 1)
            parts.append(got.reshape(in_width, 8, slab))
        high, low = halves(jnp.concatenate(parts, axis=1))
        mixed[:, pl.ds(pl.multiple_of(b * 16, 16), 16), :] = high
        mixed[:, pl.ds(pl.multiple_of(out_width + b * 16, 16), 16), :] = low
        return carry

    lax.fori_loop(0, out_width // 16, mix, 0)

    def weigh(i, carry):
        both = mm(first, mixed[i], 1, 0)
        high, low = halves(both[:out_width] + both[out_width:])
        scaled_high, scaled_low = halves(bo * scaling_ref[pl.ds(i, 1), :])
        last = jnp.concatenate(
            [
                jnp.concatenate([scaled_high, scaled_high], axis=1),
                jnp.concatenate([scaled_low, scaled_low], axis=1),
            ],
            axis=0,
        )
        both = mm(last, jnp.concatenate([high, low], axis=0), 1, 0)
        weighed[pl.ds(pl.multiple_of(i * out_width, out_width), out_width), :] = (
            both[:out_width] + both[out_width:]
        ).astype(bf16)
        return carry

    quarter = 8 * CUT

    def absorb(slot, side, limits, fresh=False, some=range(chunks)):
        code = code_got[slot]
        doc, place = code >> 16, code & (PLACES - 1)
        listed = lax.broadcasted_iota(jnp.int32, (docs, cap), 0) == doc
        limit = jnp.sum(jnp.where(listed, limits, 0.0), axis=0, keepdims=True)
        named = jnp.where(place.astype(f32) < limit, doc.astype(f32), -1.0)
        named = jnp.broadcast_to(named, (16, cap)).astype(bf16)
        grads = g_got[slot]
        for start in range(0, docs, 8):
            kept = [named == jnp.asarray(e, bf16) for e in range(start, start + 8)]
            for c in some:
                inputs = x_got[slot, pl.ds(c * CUT, CUT), :]
                spread = jnp.concatenate(
                    [jnp.where(mask, inputs, jnp.zeros_like(inputs)) for mask in kept], axis=0
                )
                rows = pl.ds(start * CUT, quarter)
                added = mm(spread, grads, 1, 0)
                if fresh:
                    acc[side, c, rows, :] = added
                else:
                    acc[side, c, rows, :] += added

    def far_copy(d, c):
        columns = pl.ds(c * span, span)
        return pltpu.make_async_remote_copy(
            feats.at[0, :, columns], feats.at[2 * d, :, columns],
            far_send.at[d, c], far_recv.at[d, c],
            device_id={"store": (chip + d) % chips * 2 + core}, device_id_type=MESH,
        )

    def near_copy(d, c):
        columns = pl.ds(c * span, span)
        return pltpu.make_async_remote_copy(
            feats.at[2 * d, :, columns], feats.at[2 * d + 1, :, columns],
            near_send.at[d, c], near_recv.at[d, c],
            device_id={"store": partner}, device_id_type=MESH,
        )

    def forward(c):
        for d in range(1, chips):
            far_copy(d, c).wait_recv()
            near_copy(d, c).start()

    def score_chip(d, c):
        columns = pl.ds(c * span, span)
        near_copy(d, c).wait_recv()
        queried = feats[pl.ds(2 * d, 2), :, columns].reshape(2 * docs, span)
        part = mm(queried, weighed[columns, :], 1, 0)
        rows = pl.ds(2 * d * docs, 2 * docs)
        if c == 0:
            total[rows, :] = part
        else:
            total[rows, :] += part

    def score(c):
        for d in range(chips):
            near_copy(d, c).wait_recv()
        columns = pl.ds(c * span, span)
        queried = feats[:, :, columns].reshape(stores * docs, span)
        part = mm(queried, weighed[columns, :], 1, 0)
        if c == 0:
            total[...] = part
        else:
            total[...] += part

    def depart(c):
        for i in range(CUT):
            feats[0, :, pl.ds(c * span + i * out_width, out_width)] = acc[
                0, c, pl.ds(i, docs, stride=CUT), :
            ].astype(bf16)
        for d in range(1, chips):
            far_copy(d, c).start()
        near_copy(0, c).start()

    limits = upright(len_ref[...].astype(f32))

    def arrive(m, side, limits):
        for copy in row_copies(m):
            copy.wait_recv()
        absorb(m, side, limits)

    g_copy.wait()
    absorb(0, 0, limits, True)
    early = in_width // 4 * 3
    lax.fori_loop(0, early, weigh, 0, unroll=8)

    @pl.when(relayed)
    def _():
        len_copy.wait_recv()
        passed = upright(len_got[...].astype(f32))
        g_pass.wait()
        absorb(half, 1, passed)
        over(queries - 1, half + 2, lambda m: arrive(m, 1, passed))
        for copy in row_copies(half + 1):
            copy.wait_recv()
        for c in range(chunks):
            absorb(half + 1, 1, passed, some=[c])
            part_out[c] = acc[1, c].astype(bf16)
            part_copy(c).start()

    lax.fori_loop(early, in_width, weigh, 0, unroll=8)
    over(half - 1, 1, lambda m: arrive(m, 0, limits))

    @pl.when(direct)
    def _():
        over(queries - 1, half, lambda m: arrive(m, 0, limits))
        for c in range(chunks):
            depart(c)
        for c in range(chunks):
            forward(c)
            if c > 0:
                score(c - 1)
        score(chunks - 1)

    @pl.when(relayed)
    def _():
        for c in range(chunks):
            part_copy(c).wait_recv()
            acc[0, c] += part_got[c].astype(f32)
            depart(c)
        for c in range(chunks - 1):
            forward(c)
            if c > 0:
                score(c - 1)
        if chunks > 1:
            score(chunks - 2)
        score_chip(0, chunks - 1)
        forward(chunks - 1)
        for d in range(1, chips):
            score_chip(d, chunks - 1)

    def put(slot, owner):
        start = pl.multiple_of(owner * docs, docs)
        out_ref[pl.ds(start, docs), :] = total[pl.ds(slot * docs, docs), :].astype(bf16)

    for d in range(chips):
        origin = (chip + chips - d) % chips * 2
        put(2 * d, origin + core)
        put(2 * d + 1, origin + (1 - core))

    def drain(m):
        for copy in row_copies(m):
            copy.wait_send()

    over(queries - 1, half + 1, drain)
    over(half - 1, 1, drain)

    @pl.when(direct)
    def _():
        drain(half)

    @pl.when(relayed)
    def _():
        len_copy.wait_send()
        for c in range(chunks):
            part_copy(c).wait_send()

    for c in range(chunks):
        for d in range(1, chips):
            far_copy(d, c).wait_send()
        for d in range(chips):
            near_copy(d, c).wait_send()


def on_device(
    queries, stores,
    in_rows, out_rows, row_doc, row_pos, doc_len, eig_in, eig_out, basis_in, basis_out, train_feats,
):
    row_count, in_width = in_rows.shape[1:]
    out_width = out_rows.shape[2]
    docs = doc_len.shape[1]
    slab, feat = train_feats.shape[1:]
    cap = row_count // queries
    hbm = pl.BlockSpec(memory_space=pltpu.HBM)
    vmem = pl.BlockSpec(memory_space=pltpu.VMEM)
    dma = pltpu.SemaphoreType.DMA
    chips = stores // 2
    chunks = in_width // CUT
    scores = pl.pallas_call(
        functools.partial(kernel, queries, stores),
        name="attribution",
        out_shape=jax.ShapeDtypeStruct((stores * docs, slab), bf16),
        in_specs=[hbm] * 10,
        out_specs=vmem,
        scratch_shapes=[
            pltpu.VMEM((1, docs), jnp.int32),
            pltpu.VMEM((1, in_width), f32),
            pltpu.VMEM((1, out_width), f32),
            pltpu.VMEM((in_width, in_width), f32),
            pltpu.VMEM((out_width, out_width), f32),
            dma((8,)),
            pltpu.VMEM((in_width, row_count), bf16),
            pltpu.VMEM((1, row_count), jnp.int32),
            pltpu.VMEM((1, row_count), jnp.int32),
            pltpu.VMEM((in_width, row_count), bf16),
            pltpu.VMEM((1, row_count), jnp.int32),
            pltpu.VMEM((queries, in_width, cap), bf16),
            pltpu.VMEM((queries, cap, out_width), bf16),
            pltpu.VMEM((queries, 1, cap), jnp.int32),
            pltpu.VMEM((1, docs), jnp.int32),
            pltpu.VMEM((slab, feat), bf16),
            pltpu.VMEM((2, chunks, docs * CUT, out_width), f32),
            pltpu.VMEM((stores, docs, feat), bf16),
            pltpu.VMEM((chunks, docs * CUT, out_width), bf16),
            pltpu.VMEM((chunks, docs * CUT, out_width), bf16),
            pltpu.VMEM((8 * in_width, 16 * in_width), bf16),
            pltpu.VMEM((in_width, out_width), f32),
            pltpu.VMEM((in_width, 2 * out_width, slab), bf16),
            pltpu.VMEM((feat, slab), bf16),
            pltpu.VMEM((stores * docs, slab), f32),
            dma((queries,)), dma((queries,)), dma((queries,)),
            dma((queries,)), dma((queries,)), dma((queries,)),
            dma((2,)), dma, dma((2,)),
            dma((chunks,)), dma((chunks,)),
            *[dma((chips, chunks))] * 4,
        ],
        compiler_params=pltpu.CompilerParams(
            collective_id=0, has_side_effects=True, vmem_limit_bytes=67043328
        ),
    )(
        in_rows[0].T, out_rows[0], row_doc, row_pos, doc_len, eig_in[None], eig_out[None], basis_in, basis_out,
        train_feats[0],
    )
    return scores[None]


def solution(mesh):
    placed = (
        P("query", "store", None),
        P("query", "store", None),
        P("query", "store"),
        P("query", "store"),
        P("query", "store"),
        P(),
        P(),
        P(),
        P(),
        P("query", "store", None),
    )
    return jax.shard_map(
        functools.partial(on_device, mesh.shape["query"], mesh.shape["store"]),
        mesh=mesh, in_specs=placed, out_specs=P("query", None, "store"), check_vma=False,
    )
```
